128 devices in a mesh: rows: 16 (over x, z), cols: 8 (over y, core).
Axes of the slice: x: 4, y: 4, z: 4, core: 2. Of those that a mesh axis runs over, the one named last changes fastest.
Arguments:
- counts: int32 [2048, 512, 512], P(('rows', 'cols')), may hold values from 0 to 1024, as said below
- shard_rows: int32 [2048], P(('rows', 'cols')), may hold values from 0 to 255, as said below
- shard_cols: int32 [2048], P(('rows', 'cols')), may hold values from 0 to 255, as said below
- listed: int32 [128], P(('rows', 'cols')), may hold values from 2 to 16, as said below
- row_embed: float32 [131072, 256], P(('rows', 'cols')), may hold values from -1.5 to 1.5
- row_accum: float32 [131072, 256], P(('rows', 'cols')), may hold values from 300 to 10000
- row_offset: bfloat16 [131072], P(('rows', 'cols')), may hold values from -3 to -1
- col_embed: float32 [131072, 256], P(('rows', 'cols')), may hold values from -1.5 to 1.5
- col_accum: float32 [131072, 256], P(('rows', 'cols')), may hold values from 300 to 10000
- col_offset: bfloat16 [131072], P(('rows', 'cols')), may hold values from -3 to -1
Outputs:
- row_trained: float32 [131072, 256], P(('rows', 'cols'))
- col_trained: float32 [131072, 256], P(('rows', 'cols'))
The draws below stay inside these ranges and needn't reach their ends.
Inputs may be any that keep to these rules, and one draw needn't show every extreme that they name: `shard_rows`: entry q belongs to holder h = q // 16, the device at rows index h // 8 and cols index h % 8. Row block g is owned by device g // 2 in the same order. The row block of a listed entry is owned by a device with its holder's cols index; the listed entries of one holder use at most 1 different row blocks of any one owner, and in some holder exactly 1 of each of the 16 owners with its cols index. `shard_cols`: column block c is owned by device c // 2. The column block of a listed entry is owned by a device with its holder's rows index. No holder lists the same pair of blocks twice. The listed entries of holder h are its first listed[h] ones; its other entries and their counts take no part. `counts`: zero where the pair of items never occurs together.
All inputs are finite; a program needn't handle non-finite values.
Results may differ from the reference program's by a relative error of at most 0.0014.
Values may be sent and summed in bfloat16 or wider, within the bound.
A program may use at most 192 MiB of HBM per device.

```python
import math
import jax
import jax.numpy as jnp
from jax import lax

D = 256
B = 512
RB_DEV = 2
CB_DEV = 2
CAP = 1
SLOTS = 16
STEPS = 1
ROW_BLOCKS = 256
COL_BLOCKS = 256
ROW_ITEMS = 131072
COL_ITEMS = 131072
N_ROWS = 16
N_COLS = 8
DEVICES = 128


def layout(key):
    holders = N_ROWS * N_COLS
    col_choices = N_COLS * CB_DEV
    wants = N_ROWS * CAP
    subkeys = jax.random.split(jax.random.fold_in(key, 7), 6)
    holder_ids = jnp.arange(holders, dtype=jnp.int32)
    forced = jax.random.randint(subkeys[0], (), 0, holders, dtype=jnp.int32)
    is_forced = holder_ids == forced
    is_sparse = holder_ids == (forced + 1) % holders
    owner_ids = jnp.arange(N_ROWS, dtype=jnp.int32)[None, :]
    anchor = owner_ids == (holder_ids % N_ROWS)[:, None]
    demand = jax.random.randint(subkeys[1], (holders, N_ROWS), 0, CAP + 1, dtype=jnp.int32)
    demand = jnp.where(anchor, jnp.maximum(demand, 1), demand)
    demand = jnp.where(is_forced[:, None], CAP, demand)
    demand = jnp.where(is_sparse[:, None], anchor.astype(jnp.int32), demand)
    noise = jax.random.randint(subkeys[2], (holders, N_ROWS, RB_DEV), 0, 2 ** 20, dtype=jnp.int32)
    ranking = jnp.argsort(noise * RB_DEV + jnp.arange(RB_DEV, dtype=jnp.int32), axis=-1, stable=True).astype(jnp.int32)
    picked = ranking[:, :, :CAP]
    usable = jnp.arange(CAP, dtype=jnp.int32)[None, None, :] < demand[:, :, None]
    owner_rank = jnp.arange(N_ROWS, dtype=jnp.int32)[None, :, None]
    set_index = (owner_rank * RB_DEV + picked).reshape(holders, wants)
    usable = usable.reshape(holders, wants).astype(jnp.int32)
    jumble = jax.random.randint(subkeys[3], (holders, wants), 0, 2 ** 20, dtype=jnp.int32)
    sort_keys = (1 - usable) * 2 ** 29 + jumble * wants + jnp.arange(wants, dtype=jnp.int32)[None, :]
    arrangement = jnp.argsort(sort_keys, axis=1, stable=True).astype(jnp.int32)
    compact = jnp.take_along_axis(set_index, arrangement, axis=1)
    distinct = jnp.sum(usable, axis=1).astype(jnp.int32)
    levels = jax.random.randint(subkeys[4], (holders,), 0, 4, dtype=jnp.int32)
    levels = jnp.where(is_sparse, 3, levels)
    listed_total = jnp.right_shift(jnp.full((holders,), SLOTS, jnp.int32), levels)
    listed_total = jnp.minimum(jnp.maximum(listed_total, distinct), distinct * col_choices)
    listed_total = jnp.where(is_forced, SLOTS, listed_total).astype(jnp.int32)
    positions = jnp.arange(SLOTS, dtype=jnp.int32)[None, :]
    row_pick = positions % distinct[:, None]
    rounds = positions // distinct[:, None]
    offsets = jax.random.randint(subkeys[5], (holders, wants), 0, col_choices, dtype=jnp.int32)
    col_pick = (rounds + jnp.take_along_axis(offsets, row_pick, axis=1)) % col_choices
    row_local = jnp.take_along_axis(compact, row_pick, axis=1)
    mesh_row = (holder_ids // N_COLS)[:, None]
    mesh_col = (holder_ids % N_COLS)[:, None]
    row_global = (row_local // RB_DEV * N_COLS + mesh_col) * RB_DEV + row_local % RB_DEV
    col_global = (mesh_row * N_COLS + col_pick // CB_DEV) * CB_DEV + col_pick % CB_DEV
    return (row_global.reshape(-1).astype(jnp.int32), col_global.reshape(-1).astype(jnp.int32), listed_total)


def draw_shard_rows(key, part):
    return layout(key)[0]


def draw_shard_cols(key, part):
    return layout(key)[1]


def draw_listed(key, part):
    return layout(key)[2]


def draw_counts(key, part):
    subkeys = jax.random.split(jax.random.fold_in(key, 11), 3)
    shape = (DEVICES * SLOTS, B, B)
    present = jax.random.randint(subkeys[0], shape, 0, 5, dtype=jnp.int32) < 3
    levels = jax.random.randint(subkeys[1], shape, 0, 11, dtype=jnp.int32)
    values = jax.random.randint(subkeys[2], shape, 1, jnp.left_shift(1, levels) + 1, dtype=jnp.int32)
    values = jnp.where(present, values, 0)
    return values.at[0, 0, 0].set(1024)


def block_scale(key, dims, shards, least, high):
    loudness, own = 1.0, jax.random.fold_in(key, 6)
    for axis_at, blocks in shards:
        heights = jnp.exp(jax.random.uniform(jax.random.fold_in(own, axis_at), (blocks,), jnp.float32, least / len(shards), high / len(shards)))
        loudness = loudness * jnp.repeat(heights, dims[axis_at] // blocks).reshape([-1 if axis == axis_at else 1 for axis in range(len(dims))])
    return loudness


def normal_values(key, extent, width, bound, cuts=(), held_as=jnp.bfloat16):
    values = jax.random.normal(key, extent, jnp.float32) * width
    if len(cuts) > 0:
        values = block_scale(key, extent, cuts, -0.22, 0.18) * values
    return jnp.clip(values, min=-bound, max=bound).astype(held_as)


def setup_inputs(seed: int = 0) -> dict:
    key_list = jax.random.split(jax.random.key(seed), 11)
    counts = draw_counts(jax.random.fold_in(key_list[10], 71), 0)
    shard_rows = draw_shard_rows(jax.random.fold_in(key_list[10], 71), 0)
    shard_cols = draw_shard_cols(jax.random.fold_in(key_list[10], 71), 0)
    listed = draw_listed(jax.random.fold_in(key_list[10], 71), 0)
    row_embed = normal_values(key_list[4], (ROW_ITEMS, D), 0.25, 1.5, ((0, 128),), jnp.float32)
    row_accum = jnp.clip(jnp.exp(math.log(10000.0) - 3.506558 * jax.random.uniform(key_list[5], (ROW_ITEMS, D), jnp.float32) ** block_scale(key_list[5], (ROW_ITEMS, D), ((0, 128),), -0.2, 0.2)), 300.0, 10000.0)
    row_offset = jnp.clip(-3.0 + 2.0 * jax.random.uniform(key_list[6], (ROW_ITEMS,), jnp.float32) ** block_scale(key_list[6], (ROW_ITEMS,), ((0, 128),), -0.2, 0.2), -3.0, -1.0).astype(jnp.bfloat16)
    col_embed = normal_values(key_list[7], (COL_ITEMS, D), 0.25, 1.5, ((0, 128),), jnp.float32)
    col_accum = jnp.clip(jnp.exp(math.log(10000.0) - 3.506558 * jax.random.uniform(key_list[8], (COL_ITEMS, D), jnp.float32) ** block_scale(key_list[8], (COL_ITEMS, D), ((0, 128),), -0.2, 0.2)), 300.0, 10000.0)
    col_offset = jnp.clip(-3.0 + 2.0 * jax.random.uniform(key_list[9], (COL_ITEMS,), jnp.float32) ** block_scale(key_list[9], (COL_ITEMS,), ((0, 128),), -0.2, 0.2), -3.0, -1.0).astype(jnp.bfloat16)
    return dict(counts=counts, shard_rows=shard_rows, shard_cols=shard_cols, listed=listed, row_embed=row_embed, row_accum=row_accum, row_offset=row_offset, col_embed=col_embed, col_accum=col_accum, col_offset=col_offset)


learning_rate = 0.5
conf_base = 0.1
conf_scale = 0.25

def slopes(cell_counts, scores, row_shift, col_shift):
    floored = jnp.maximum(cell_counts, 1).astype(jnp.float32)
    pointwise = jnp.log(floored) + row_shift[:, :, None] + col_shift[:, None, :]
    weight = conf_base + conf_scale * jnp.sqrt(floored)
    return jnp.where(cell_counts > 0, weight * (scores - pointwise), jax.nn.sigmoid(scores - pointwise))

def reference(counts, shard_rows, shard_cols, listed, row_embed, row_accum, row_offset, col_embed, col_accum, col_offset):
    holders = N_ROWS * N_COLS
    tile_sets = counts.reshape(holders, SLOTS, B, B)
    row_lists = shard_rows.reshape(holders, SLOTS)
    col_lists = shard_cols.reshape(holders, SLOTS)
    live_slots = jnp.arange(SLOTS, dtype=jnp.int32)[None, :] < listed[:, None]
    row_shifts = row_offset.astype(jnp.float32).reshape(ROW_BLOCKS, B)
    col_shifts = col_offset.astype(jnp.float32).reshape(COL_BLOCKS, B)
    for repeat in range(STEPS):
        row_half = lax.optimization_barrier(row_embed.astype(jnp.bfloat16)).reshape(ROW_BLOCKS, B, D)
        col_half = lax.optimization_barrier(col_embed.astype(jnp.bfloat16)).reshape(COL_BLOCKS, B, D)

        def holder_terms(totals, inputs):
            row_grad, col_grad = totals
            tile_group, row_ids, col_ids, in_list = inputs
            row_vectors = row_half[row_ids].astype(jnp.float32)
            col_vectors = col_half[col_ids].astype(jnp.float32)
            scores = jnp.einsum('sbd,sed->sbe', row_vectors, col_vectors, precision=lax.Precision.HIGHEST)
            slope_full = slopes(tile_group, scores, row_shifts[row_ids], col_shifts[col_ids])
            slope_full = jnp.where(in_list[:, None, None], slope_full, jnp.zeros_like(slope_full))
            slope_half = lax.optimization_barrier(slope_full.astype(jnp.bfloat16)).astype(jnp.float32)
            row_terms = jnp.einsum('sbe,sed->sbd', slope_half, col_vectors, precision=lax.Precision.HIGHEST)
            col_terms = jnp.einsum('sbe,sbd->sed', slope_half, row_vectors, precision=lax.Precision.HIGHEST)
            return ((row_grad.at[row_ids].add(row_terms), col_grad.at[col_ids].add(col_terms)), None)
        start = (jnp.zeros((ROW_BLOCKS, B, D), jnp.float32), jnp.zeros((COL_BLOCKS, B, D), jnp.float32))
        (row_grad, col_grad), unused = lax.scan(holder_terms, start, (tile_sets, row_lists, col_lists, live_slots))
        row_grad = row_grad.reshape(ROW_ITEMS, D)
        col_grad = col_grad.reshape(COL_ITEMS, D)
        row_accum = row_accum + row_grad * row_grad
        col_accum = col_accum + col_grad * col_grad
        row_embed = row_embed - learning_rate * row_grad / jnp.sqrt(row_accum)
        col_embed = col_embed - learning_rate * col_grad / jnp.sqrt(col_accum)
    return (row_embed, col_embed)
```

```python
import functools

import jax
import jax.numpy as jnp
from jax import lax
from jax.experimental import pallas as pl
from jax.experimental.pallas import tpu as pltpu
from jax.sharding import PartitionSpec as P

learning_rate = 0.5
conf_base = 0.1
conf_scale = 0.25
SIDE = 4
PAD = 16
FLOOR = 1.0 / 16.0
CODE = 32766.0 / 30.0
MESH = pl.DeviceIdType.MESH
ANY = pl.BlockSpec(memory_space=pl.ANY)


def encode(term):
    level = jnp.log2(1.0 + jnp.abs(term) * (1.0 / FLOOR)) * CODE + 0.5
    whole = level.astype(jnp.int32)
    return jnp.where(term < 0.0, -whole, whole).astype(jnp.int16)


def decode(code):
    level = code.astype(jnp.int32).astype(jnp.float32)
    size = jnp.exp2(jnp.abs(level) * (1.0 / CODE)) * FLOOR - FLOOR
    return jnp.where(level < 0.0, -size, size)


def place():
    row, col = lax.axis_index("rows"), lax.axis_index("cols")
    return row // SIDE, row % SIDE, col // 2, col % 2


def device(x, y, z, core):
    return (x * SIDE + z, y * 2 + core)


def turn(at, by):
    return lax.rem(at + (by + SIDE), SIDE)


class Copies:
    def __init__(self, send_sems, recv_sems):
        self.send_sems, self.recv_sems, self.started = send_sems, recv_sems, []

    def start(self, source, target, to):
        at = len(self.started)
        copy = pltpu.make_async_remote_copy(
            src_ref=source,
            dst_ref=target,
            send_sem=self.send_sems.at[at],
            recv_sem=self.recv_sems.at[at],
            device_id=to,
            device_id_type=MESH,
        )
        copy.start()
        self.started.append(copy)
        return copy

    def finish(self):
        for copy in self.started:
            copy.wait_send()


def greet(peers):
    barrier = pltpu.get_barrier_semaphore()
    for peer in peers:
        pl.semaphore_signal(barrier, inc=1, device_id=peer, device_id_type=MESH)
    pl.semaphore_wait(barrier, len(peers))


def gather_kernel(row_ref, col_ref, sel_ref, row_pool, col_pool, sel_in, send_sems, recv_sems, local_sems):
    x, z, y, core = place()
    row, col = lax.axis_index("rows"), lax.axis_index("cols")
    block_items = row_ref.shape[1] - PAD
    parts = (pl.ds(0, block_items // 2), pl.ds(block_items // 2, block_items // 2 + PAD))
    others = [(dx, dz) for dx in range(SIDE) for dz in range(SIDE) if (dx, dz) != (0, 0)]
    far = [device(turn(x, dx), y, turn(z, dz), core) for dx, dz in others]
    along_y = [device(x, turn(y, d), z, core) for d in (1, -1)]
    partner = device(x, y, z, 1 - core)
    greet(far + along_y + [partner])
    net = Copies(send_sems, recv_sems)

    own_row = pltpu.make_async_copy(row_ref, row_pool.at[row], local_sems.at[0])
    own_col = pltpu.make_async_copy(col_ref, col_pool.at[col], local_sems.at[1])

    def hop(axis, by):
        if axis == 0:
            return device(turn(x, by), y, z, core)
        return device(x, y, turn(z, by), core)

    def pool(block, first, second, part=None):
        dx, dz = (first, second) if block == 0 else (second, first)
        ref = row_pool.at[turn(x, dx) * SIDE + turn(z, dz), block]
        return ref if part is None else ref.at[parts[part]]

    def own(block, part=None):
        ref = row_ref.at[block]
        return ref if part is None else ref.at[parts[part]]

    axes = ((0, 1), (1, 0))
    one, two, relay_one, relay_two = {}, {}, {}, {}
    for block in (0, 1):
        for by in (1, -1):
            one[block, by] = net.start(own(block), pool(block, 0, 0), hop(axes[block][0], by))
    y_own = [net.start(col_ref, col_pool.at[col], to) for to in along_y]
    core_own = net.start(col_ref, col_pool.at[col], partner)
    for block in (0, 1):
        for by in (1, -1):
            two[block, 0, by] = net.start(own(block), pool(block, 0, 0), hop(axes[block][1], by))
    own_row.start()
    own_col.start()
    chosen = [
        net.start(sel_ref.at[turn(x, dx) * SIDE + turn(z, dz)], sel_in.at[row], to)
        for (dx, dz), to in zip(others, far)
    ]
    for by in (1, -1):
        for block in (0, 1):
            one[block, by].wait_recv()
            part = 0 if by == 1 else 1
            relay_one[block, by] = net.start(
                pool(block, -by, 0, part), pool(block, -by, 0, part), hop(axes[block][0], by)
            )
            for way in (1, -1):
                two[block, -by, way] = net.start(
                    pool(block, -by, 0), pool(block, -by, 0), hop(axes[block][1], way)
                )
    col_of = lambda d: turn(y, d) * 2 + core
    to_core, relay_y = [], []
    for at, by in enumerate((1, -1)):
        y_own[at].wait_recv()
        half = 0 if by == 1 else 1
        source = col_pool.at[col_of(-by), half]
        relay_y.append(net.start(source, source, along_y[at]))
        to_core.append(net.start(col_pool.at[col_of(-by)], col_pool.at[col_of(-by)], partner))

    def second_relays(first):
        for by in (1, -1):
            for block in (0, 1):
                two[block, first, by].wait_recv()
                part = 0 if by == 1 else 1
                relay_two[block, first, by] = net.start(
                    pool(block, first, -by, part), pool(block, first, -by, part), hop(axes[block][1], by)
                )

    second_relays(0)
    for block in (0, 1):
        for by in (1, -1):
            relay_one[block, by].wait_recv()
        for way in (1, -1):
            two[block, 2, way] = net.start(pool(block, 2, 0), pool(block, 2, 0), hop(axes[block][1], way))
    for copy in relay_y:
        copy.wait_recv()
    to_core.append(net.start(col_pool.at[col_of(2)], col_pool.at[col_of(2)], partner))
    for first in (-1, 1, 2):
        second_relays(first)
    for copy in relay_two.values():
        copy.wait_recv()
    for copy in [core_own] + to_core + chosen:
        copy.wait_recv()
    net.finish()
    own_row.wait()
    own_col.wait()


GATHER_COPIES = 40 + 2 + 1 + 2 + 3 + 15


def gather(row_packed, col_packed, chosen):
    blocks, tall, features = row_packed.shape
    owners, around = SIDE * SIDE, SIDE * 2
    return pl.pallas_call(
        gather_kernel,
        out_shape=(
            jax.ShapeDtypeStruct((owners,) + row_packed.shape, jnp.bfloat16),
            jax.ShapeDtypeStruct((around,) + col_packed.shape, jnp.bfloat16),
            jax.ShapeDtypeStruct(chosen.shape, jnp.int32),
        ),
        in_specs=[ANY] * 3,
        out_specs=(ANY,) * 3,
        scratch_shapes=[
            pltpu.SemaphoreType.DMA((GATHER_COPIES,)),
            pltpu.SemaphoreType.DMA((GATHER_COPIES,)),
            pltpu.SemaphoreType.DMA((2,)),
        ],
        compiler_params=pltpu.CompilerParams(collective_id=0, has_side_effects=True),
        name="gather_blocks",
    )(row_packed, col_packed, chosen)


LIVE, SLOT, OWNER, ROW, COL, ROW_FIRST, COL_FIRST, COL_USED = range(8)


def slots_kernel(plan, counts_ref, row_ref, col_ref, row_out, col_out, row_sum, col_sum, slope_ref):
    at = pl.program_id(0)
    block_items, features = row_sum.shape
    group = min(128, block_items)

    def offsets(ref):
        wide = ref[0, block_items:, :].astype(jnp.float32)
        pieces = [wide[i : i + 1] for i in range(block_items // features)]
        return pieces[0] if len(pieces) == 1 else jnp.concatenate(pieces, axis=1)

    @pl.when(at < plan[LIVE, 0])
    def _():
        col_vectors = col_ref[0, :block_items, :]
        row_shift = jnp.broadcast_to(offsets(row_ref), (8, block_items)).T[:, :1]
        col_shift = offsets(col_ref)
        for first in range(0, block_items, group):
            rows = slice(first, first + group)
            scores = lax.dot_general(
                row_ref[0, rows, :], col_vectors, (((1,), (1,)), ((), ())), preferred_element_type=jnp.float32
            )
            cells = counts_ref[0, rows, :].astype(jnp.float32)
            floored = jnp.maximum(cells, 1.0)
            gap = scores - row_shift[rows] - col_shift - jnp.log(floored)
            weight = conf_base + conf_scale * (floored * lax.rsqrt(floored))
            slope = jnp.where(cells > 0.0, weight * gap, 0.5 * jnp.tanh(0.5 * gap) + 0.5)
            slope_ref[rows, :] = slope.astype(jnp.bfloat16)
        slope = slope_ref[...]
        row_term = jnp.dot(slope, col_vectors, preferred_element_type=jnp.float32)

        @pl.when(plan[ROW_FIRST, at] == 1)
        def _():
            row_sum[...] = row_term

        @pl.when(plan[ROW_FIRST, at] == 0)
        def _():
            row_sum[...] += row_term

        @pl.when(plan[ROW_FIRST, at + 1] == 1)
        def _():
            row_out[0] = encode(row_sum[...])

        col_term = lax.dot_general(
            row_ref[0, :block_items, :], slope, (((0,), (0,)), ((), ())), preferred_element_type=jnp.float32
        )
        which = plan[COL, at]

        @pl.when(plan[COL_FIRST, at] == 1)
        def _():
            col_sum[which] = col_term

        @pl.when(plan[COL_FIRST, at] == 0)
        def _():
            col_sum[which] += col_term

    @pl.when(at == pl.num_programs(0) - 1)
    def _():
        def one(which, carry):
            @pl.when(plan[COL_USED, which] == 1)
            def _():
                col_out[which] = encode(col_sum[which])

            @pl.when(plan[COL_USED, which] == 0)
            def _():
                col_out[which] = jnp.zeros(col_out.shape[1:], jnp.int16)

            return carry

        lax.fori_loop(0, col_out.shape[0], one, 0)


def slots(plan, counts, row_pool, col_pool):
    count, block_items, unused = counts.shape
    owners, row_blocks, tall, features = row_pool.shape
    row_pool = row_pool.reshape(-1, tall, features)
    col_pool = col_pool.reshape(-1, tall, features)
    col_blocks = col_pool.shape[0]
    grid_spec = pltpu.PrefetchScalarGridSpec(
        num_scalar_prefetch=1,
        grid=(count,),
        in_specs=[
            pl.BlockSpec((1, block_items, block_items), lambda i, plan: (plan[SLOT, i], 0, 0)),
            pl.BlockSpec((1, tall, features), lambda i, plan: (plan[ROW, i], 0, 0)),
            pl.BlockSpec((1, tall, features), lambda i, plan: (plan[COL, i], 0, 0)),
        ],
        out_specs=(
            pl.BlockSpec((1, block_items, features), lambda i, plan: (plan[OWNER, i], 0, 0)),
            pl.BlockSpec((col_blocks, features, block_items), lambda i, plan: (0, 0, 0)),
        ),
        scratch_shapes=[
            pltpu.VMEM((block_items, features), jnp.float32),
            pltpu.VMEM((col_blocks, features, block_items), jnp.float32),
            pltpu.VMEM((block_items, block_items), jnp.bfloat16),
        ],
    )
    return pl.pallas_call(
        slots_kernel,
        out_shape=(
            jax.ShapeDtypeStruct((owners, block_items, features), jnp.int16),
            jax.ShapeDtypeStruct((col_blocks, features, block_items), jnp.int16),
        ),
        grid_spec=grid_spec,
        compiler_params=pltpu.CompilerParams(dimension_semantics=("arbitrary",)),
        name="slot_terms",
    )(plan, counts, row_pool, col_pool)


def exchange_kernel(row_terms, col_terms, row_in, col_in, stage, relay_one, relay_two, relay_y, send_sems, recv_sems, local_sems):
    x, z, y, core = place()
    half = row_terms.shape[2] // 2
    ring = [device(turn(x, d), y, z, core) for d in (1, -1)] + [device(x, y, turn(z, d), core) for d in (1, -1)]
    near_y = [device(x, turn(y, d), z, k) for d in (1, -1) for k in (0, 1)]
    partner = device(x, y, z, 1 - core)
    greet(ring + near_y + [partner])
    net = Copies(send_sems, recv_sems)
    here = ((x, z), (z, x))
    low, high = pl.ds(0, 2), pl.ds(2, 2)

    def rows_of(ref, way, first, second):
        piece = pl.ds(way * half, half)
        if way == 0:
            return ref.at[first, second, piece]
        return ref.at[second, first, piece]

    def to(way, stage_number, by):
        axis = way if stage_number == 0 else 1 - way
        if axis == 0:
            return device(turn(x, by), y, z, core)
        return device(x, y, turn(z, by), core)

    whole = pl.ds(0, SIDE)
    relayed, direct, passed, second, second_relay, second_pass, local = {}, {}, {}, {}, {}, {}, []
    for way in (0, 1):
        p, q = here[way]
        for by, pick in ((1, low), (-1, high)):
            relayed[way, by] = net.start(
                rows_of(row_terms, way, turn(p, 2), pick),
                relay_one.at[way, 0 if by == 1 else 1],
                to(way, 0, by),
            )
    y_relay = {}
    for at, by in enumerate((1, -1)):
        y_relay[by] = net.start(col_terms.at[turn(y, 2), whole_core(), at], relay_y.at[at], device(x, turn(y, by), z, core))
    for way in (0, 1):
        p, q = here[way]
        for by in (1, -1):
            direct[way, by] = net.start(
                rows_of(row_terms, way, turn(p, by), whole), stage.at[way, p], to(way, 0, by)
            )
    y_direct = []
    for by in (1, -1):
        for flip in (0, 1):
            k = lax.rem(core + flip, 2)
            y_direct.append(
                net.start(col_terms.at[turn(y, by), k], col_in.at[y, core], device(x, turn(y, by), z, k))
            )
    y_direct.append(net.start(col_terms.at[y, 1 - core], col_in.at[y, core], partner))

    def second_axis(way, origin, source):
        p, q = here[way]
        place_first = turn(p, origin)
        by_far = 1 if origin in (0, -1) else -1
        key = (way, origin)
        second_relay[key] = net.start(source(turn(q, 2)), relay_two.at[way, place_first], to(way, 1, by_far))
        for by in (1, -1):
            second[key + (by,)] = net.start(
                source(turn(q, by)), rows_of(row_in, way, place_first, q), to(way, 1, by)
            )
        if origin != 0:
            copy = pltpu.make_async_copy(source(q), rows_of(row_in, way, place_first, q), local_sems.at[len(local)])
            copy.start()
            local.append(copy)

    for way in (0, 1):
        p, q = here[way]
        second_axis(way, 0, lambda at, way=way, p=p: rows_of(row_terms, way, p, at))
    for way in (0, 1):
        p, q = here[way]
        for by, pick in ((1, low), (-1, high)):
            relayed[way, by].wait_recv()
            passed[way, by] = net.start(
                relay_one.at[way, 0 if by == 1 else 1], stage.at[way, turn(p, -by), pick], to(way, 0, by)
            )
    y_pass = []
    for at, by in enumerate((1, -1)):
        y_relay[by].wait_recv()
        for flip in (0, 1):
            k = lax.rem(core + flip, 2)
            y_pass.append(
                net.start(relay_y.at[at, k], col_in.at[turn(y, -by), core, at], device(x, turn(y, by), z, k))
            )

    def pass_on(origin):
        for way in (0, 1):
            p, q = here[way]
            by = 1 if origin in (0, -1) else -1
            second_relay[way, origin].wait_recv()
            place_first = turn(p, origin)
            second_pass[way, origin] = net.start(
                relay_two.at[way, place_first], rows_of(row_in, way, place_first, turn(q, -by)), to(way, 1, by)
            )

    for by in (1, -1):
        for way in (0, 1):
            p, q = here[way]
            direct[way, by].wait_recv()
            second_axis(way, -by, lambda at, way=way, p=p, by=by: stage.at[way, turn(p, -by), at])
    pass_on(0)
    for way in (0, 1):
        p, q = here[way]
        for by in (1, -1):
            passed[way, by].wait_recv()
        second_axis(way, 2, lambda at, way=way, p=p: stage.at[way, turn(p, 2), at])
    for origin in (-1, 1, 2):
        pass_on(origin)
    for copy in list(second.values()) + list(second_pass.values()) + y_direct + y_pass:
        copy.wait_recv()
    net.finish()
    for copy in local:
        copy.wait()


def whole_core():
    return pl.ds(0, 2)


EXCHANGE_COPIES = 2 * 22 + 2 + 5 + 4


def exchange(row_terms, col_terms):
    block_items, features = row_terms.shape[2:]
    half = block_items // 2
    return pl.pallas_call(
        exchange_kernel,
        out_shape=(
            jax.ShapeDtypeStruct(row_terms.shape, jnp.int16),
            jax.ShapeDtypeStruct(col_terms.shape, jnp.int16),
        ),
        in_specs=[ANY] * 2,
        out_specs=(ANY,) * 2,
        scratch_shapes=[
            pltpu.VMEM((2, SIDE, SIDE, half, features), jnp.int16),
            pltpu.VMEM((2, 2, 2, half, features), jnp.int16),
            pltpu.VMEM((2, SIDE, half, features), jnp.int16),
            pltpu.VMEM((2, 2) + col_terms.shape[3:], jnp.int16),
            pltpu.SemaphoreType.DMA((EXCHANGE_COPIES,)),
            pltpu.SemaphoreType.DMA((EXCHANGE_COPIES,)),
            pltpu.SemaphoreType.DMA((6,)),
        ],
        compiler_params=pltpu.CompilerParams(collective_id=1, has_side_effects=True),
        name="exchange_terms",
    )(row_terms, col_terms)


def update_kernel(
    where, sel_ref, row_in, row_own, col_in, col_own, row_embed, row_accum, col_embed, col_accum,
    row_out, col_out, row_sum, col_sum,
):
    row, col = where[0], where[1]
    row_sum[...] = jnp.zeros_like(row_sum)

    def add(source, code, block):
        @pl.when(block < row_sum.shape[0])
        def _():
            row_sum[block] += decode(code)

    def one(source, carry):
        @pl.when(source != row)
        def _():
            add(source, row_in[source], sel_ref[source, 0, 0])

        return carry

    lax.fori_loop(0, row_in.shape[0], one, 0)
    add(row, row_own[0], where[2])
    col_sum[...] = decode(col_own[0])

    def other(source, carry):
        @pl.when(source != col)
        def _():
            col_sum[...] += decode(col_in[source])

        return carry

    lax.fori_loop(0, col_in.shape[0], other, 0)

    def step(embed, accum, grad, out, block):
        total = accum[block] + grad * grad
        out[block] = embed[block] - (learning_rate * grad) * lax.rsqrt(total)

    for block in range(row_sum.shape[0]):
        step(row_embed, row_accum, row_sum[block], row_out, block)
        step(col_embed, col_accum, col_sum[block].T, col_out, block)


def update(where, sel_in, row_in, row_terms, col_in, col_terms, row_embed, row_accum, col_embed, col_accum):
    blocks, block_items, features = row_embed.shape
    owners, around = row_in.shape[0], col_in.shape[0]
    group = min(128, block_items)
    state = pl.BlockSpec((blocks, group, features), lambda i, where: (0, i, 0))
    shape = jax.ShapeDtypeStruct(row_embed.shape, jnp.float32)
    grid_spec = pltpu.PrefetchScalarGridSpec(
        num_scalar_prefetch=1,
        grid=(block_items // group,),
        in_specs=[
            pl.BlockSpec(memory_space=pltpu.SMEM),
            pl.BlockSpec((owners, group, features), lambda i, where: (0, i, 0)),
            pl.BlockSpec((1, group, features), lambda i, where: (where[0], i, 0)),
            pl.BlockSpec((around, blocks, features, group), lambda i, where: (0, 0, 0, i)),
            pl.BlockSpec((1, blocks, features, group), lambda i, where: (where[1], 0, 0, i)),
        ]
        + [state] * 4,
        out_specs=(state, state),
        scratch_shapes=[
            pltpu.VMEM((blocks, group, features), jnp.float32),
            pltpu.VMEM((blocks, features, group), jnp.float32),
        ],
    )
    return pl.pallas_call(
        update_kernel,
        out_shape=(shape, shape),
        grid_spec=grid_spec,
        compiler_params=pltpu.CompilerParams(dimension_semantics=("arbitrary",)),
        name="adagrad",
    )(where, sel_in, row_in, row_terms, col_in, col_terms, row_embed, row_accum, col_embed, col_accum)


def pack(embed, offset, block_items):
    features = embed.shape[1]
    blocks = embed.shape[0] // block_items
    half = embed.astype(jnp.bfloat16).reshape(blocks, block_items, features)
    shift = offset.reshape(blocks, block_items // features, features)
    shift = jnp.pad(shift, ((0, 0), (0, PAD - block_items // features), (0, 0)))
    return jnp.concatenate([half, shift], axis=1)


def make_plan(shard_rows, shard_cols, live, row_blocks, col_blocks):
    around, owners = SIDE * 2, SIDE * SIDE
    slots_count = shard_rows.shape[0]
    at = jnp.arange(slots_count, dtype=jnp.int32)
    listed = at < live
    owner = shard_rows // row_blocks // around
    block = shard_rows % row_blocks
    row = owner * row_blocks + block
    col = shard_cols // col_blocks % around * col_blocks + shard_cols % col_blocks
    key = jnp.where(listed, owner, owners) * slots_count + at
    rank = jnp.sum((key[None, :] < key[:, None]).astype(jnp.int32), axis=1)
    takes = (rank[None, :] == jnp.minimum(at, live - 1)[:, None]).astype(jnp.int32)
    ordered = jnp.sum(takes[None] * jnp.stack([at, owner, row, col])[:, None, :], axis=2)
    slot, owner_at, row_at, col_at = ordered
    real = listed
    row_first = jnp.where((at == 0) | (owner_at != jnp.roll(owner_at, 1)) | (at >= live), 1, 0)
    earlier = (col_at[None, :] == col_at[:, None]) & (at[None, :] < at[:, None])
    col_first = 1 - jnp.any(earlier, axis=1).astype(jnp.int32)
    ids = jnp.arange(around * col_blocks, dtype=jnp.int32)
    col_used = jnp.any((ids[:, None] == col[None, :]) & listed[None, :], axis=1).astype(jnp.int32)
    rows = [jnp.full((slots_count,), live, jnp.int32), slot, owner_at, row_at, col_at, row_first, col_first]
    plan = jnp.stack(rows)
    plan = jnp.pad(plan, ((0, 0), (0, 1)), constant_values=1)
    plan = jnp.concatenate([plan, jnp.pad(col_used, (0, slots_count + 1 - col_used.shape[0]))[None]], axis=0)
    ids = jnp.arange(owners, dtype=jnp.int32)
    mine = (owner[None, :] == ids[:, None]) & listed[None, :]
    chosen = jnp.min(jnp.where(mine, block[None, :], row_blocks), axis=1)
    return plan, chosen


def on_device(
    counts, shard_rows, shard_cols, listed, row_embed, row_accum, row_offset, col_embed, col_accum, col_offset
):
    block_items = counts.shape[1]
    features = row_embed.shape[1]
    row_blocks = row_embed.shape[0] // block_items
    col_blocks = col_embed.shape[0] // block_items
    row, col = lax.axis_index("rows"), lax.axis_index("cols")
    plan, chosen = make_plan(shard_rows, shard_cols, listed[0], row_blocks, col_blocks)
    row_packed = pack(row_embed, row_offset, block_items)
    col_packed = pack(col_embed, col_offset, block_items)
    tiles = jnp.broadcast_to(chosen[:, None, None], (SIDE * SIDE, 8, 128))
    row_pool, col_pool, sel_in = gather(row_packed, col_packed, tiles)
    row_terms, col_terms = slots(plan, counts, row_pool, col_pool)
    row_in, col_in = exchange(
        row_terms.reshape(SIDE, SIDE, block_items, features),
        col_terms.reshape(SIDE, 2, col_blocks, features, block_items),
    )
    where = jnp.stack([row, col, jnp.sum(jnp.where(jnp.arange(SIDE * SIDE) == row, chosen, 0))]).astype(jnp.int32)
    row_state = (row_blocks, block_items, features)
    col_state = (col_blocks, block_items, features)
    row_new, col_new = update(
        where,
        sel_in,
        row_in.reshape(row_terms.shape),
        row_terms,
        col_in.reshape(SIDE * 2, col_blocks, features, block_items),
        col_terms.reshape(SIDE * 2, col_blocks, features, block_items),
        row_embed.reshape(row_state),
        row_accum.reshape(row_state),
        col_embed.reshape(col_state),
        col_accum.reshape(col_state),
    )
    return (row_new.reshape(row_embed.shape), col_new.reshape(col_embed.shape))


def solution(mesh):
    devices = ("rows", "cols")
    in_specs = (P(devices, None, None), P(devices), P(devices), P(devices)) + (
        P(devices, None),
        P(devices, None),
        P(devices),
    ) * 2
    out_specs = (P(devices, None), P(devices, None))
    return jax.shard_map(on_device, mesh=mesh, in_specs=in_specs, out_specs=out_specs, check_vma=False)
```

```python
import functools

import jax
import jax.numpy as jnp
from jax import lax
from jax.experimental import pallas as pl
from jax.experimental.pallas import tpu as pltpu
from jax.sharding import PartitionSpec as P

learning_rate = 0.5
conf_base = 0.1
conf_scale = 0.25
SIDE = 4
PAD = 16
FLOOR = 1.0 / 16.0
CODE = 32766.0 / 30.0
MESH = pl.DeviceIdType.MESH
ANY = pl.BlockSpec(memory_space=pl.ANY)


def encode(term):
    level = jnp.log2(1.0 + jnp.abs(term) * (1.0 / FLOOR)) * CODE + 0.5
    whole = level.astype(jnp.int32)
    return jnp.where(term < 0.0, -whole, whole).astype(jnp.int16)


def decode(code):
    level = code.astype(jnp.int32).astype(jnp.float32)
    size = jnp.exp2(jnp.abs(level) * (1.0 / CODE)) * FLOOR - FLOOR
    return jnp.where(level < 0.0, -size, size)


def place():
    row, col = lax.axis_index("rows"), lax.axis_index("cols")
    return row // SIDE, row % SIDE, col // 2, col % 2


def device(x, y, z, core):
    return (x * SIDE + z, y * 2 + core)


def turn(at, by):
    return lax.rem(at + (by + SIDE), SIDE)


class Copies:
    def __init__(self, send_sems, recv_sems):
        self.send_sems, self.recv_sems, self.started = send_sems, recv_sems, []

    def start(self, source, target, to):
        at = len(self.started)
        copy = pltpu.make_async_remote_copy(
            src_ref=source,
            dst_ref=target,
            send_sem=self.send_sems.at[at],
            recv_sem=self.recv_sems.at[at],
            device_id=to,
            device_id_type=MESH,
        )
        copy.start()
        self.started.append(copy)
        return copy

    def finish(self):
        for copy in self.started:
            copy.wait_send()


def greet(peers):
    barrier = pltpu.get_barrier_semaphore()
    for peer in peers:
        pl.semaphore_signal(barrier, inc=1, device_id=peer, device_id_type=MESH)
    pl.semaphore_wait(barrier, len(peers))


def gather_kernel(row_ref, col_ref, sel_ref, row_pool, col_pool, sel_in, send_sems, recv_sems, local_sems):
    x, z, y, core = place()
    row, col = lax.axis_index("rows"), lax.axis_index("cols")
    block_items = row_ref.shape[1] - PAD
    parts = (pl.ds(0, block_items // 2), pl.ds(block_items // 2, block_items // 2 + PAD))
    others = [(dx, dz) for dx in range(SIDE) for dz in range(SIDE) if (dx, dz) != (0, 0)]
    far = [device(turn(x, dx), y, turn(z, dz), core) for dx, dz in others]
    along_y = [device(x, turn(y, d), z, core) for d in (1, -1)]
    partner = device(x, y, z, 1 - core)
    greet(far + along_y + [partner])
    net = Copies(send_sems, recv_sems)

    own_row = pltpu.make_async_copy(row_ref, row_pool.at[row], local_sems.at[0])
    own_col = pltpu.make_async_copy(col_ref, col_pool.at[col], local_sems.at[1])
    own_sel = pltpu.make_async_copy(sel_ref, sel_in.at[row], local_sems.at[2])

    def hop(axis, by):
        if axis == 0:
            return device(turn(x, by), y, z, core)
        return device(x, y, turn(z, by), core)

    def pool(block, first, second, part=None):
        dx, dz = (first, second) if block == 0 else (second, first)
        ref = row_pool.at[turn(x, dx) * SIDE + turn(z, dz), block]
        return ref if part is None else ref.at[parts[part]]

    def own(block, part=None):
        ref = row_ref.at[block]
        return ref if part is None else ref.at[parts[part]]

    axes = ((0, 1), (1, 0))
    one, two, relay_one, relay_two = {}, {}, {}, {}
    for block in (0, 1):
        for by in (1, -1):
            one[block, by] = net.start(own(block), pool(block, 0, 0), hop(axes[block][0], by))
    y_own = [net.start(col_ref, col_pool.at[col], to) for to in along_y]
    core_own = net.start(col_ref, col_pool.at[col], partner)
    for block in (0, 1):
        for by in (1, -1):
            two[block, 0, by] = net.start(own(block), pool(block, 0, 0), hop(axes[block][1], by))
    own_row.start()
    own_col.start()
    own_sel.start()
    chosen = [
        net.start(sel_ref, sel_in.at[row], to) for to in far
    ]
    for by in (1, -1):
        for block in (0, 1):
            one[block, by].wait_recv()
            part = 0 if by == 1 else 1
            relay_one[block, by] = net.start(
                pool(block, -by, 0, part), pool(block, -by, 0, part), hop(axes[block][0], by)
            )
            for way in (1, -1):
                two[block, -by, way] = net.start(
                    pool(block, -by, 0), pool(block, -by, 0), hop(axes[block][1], way)
                )
    col_of = lambda d: turn(y, d) * 2 + core
    to_core, relay_y = [], []
    for at, by in enumerate((1, -1)):
        y_own[at].wait_recv()
        half = 0 if by == 1 else 1
        source = col_pool.at[col_of(-by), half]
        relay_y.append(net.start(source, source, along_y[at]))
        to_core.append(net.start(col_pool.at[col_of(-by)], col_pool.at[col_of(-by)], partner))

    def second_relays(first):
        for by in (1, -1):
            for block in (0, 1):
                two[block, first, by].wait_recv()
                part = 0 if by == 1 else 1
                relay_two[block, first, by] = net.start(
                    pool(block, first, -by, part), pool(block, first, -by, part), hop(axes[block][1], by)
                )

    second_relays(0)
    for block in (0, 1):
        for by in (1, -1):
            relay_one[block, by].wait_recv()
        for way in (1, -1):
            two[block, 2, way] = net.start(pool(block, 2, 0), pool(block, 2, 0), hop(axes[block][1], way))
    for copy in relay_y:
        copy.wait_recv()
    to_core.append(net.start(col_pool.at[col_of(2)], col_pool.at[col_of(2)], partner))
    for first in (-1, 1, 2):
        second_relays(first)
    for copy in relay_two.values():
        copy.wait_recv()
    for copy in [core_own] + to_core + chosen:
        copy.wait_recv()
    net.finish()
    own_row.wait()
    own_col.wait()
    own_sel.wait()


GATHER_COPIES = 40 + 2 + 1 + 2 + 3 + 15


def gather(row_packed, col_packed, sel):
    blocks, tall, features = row_packed.shape
    owners, around = SIDE * SIDE, SIDE * 2
    return pl.pallas_call(
        gather_kernel,
        out_shape=(
            jax.ShapeDtypeStruct((owners,) + row_packed.shape, jnp.bfloat16),
            jax.ShapeDtypeStruct((around,) + col_packed.shape, jnp.bfloat16),
            jax.ShapeDtypeStruct((owners,) + sel.shape, jnp.int32),
        ),
        in_specs=[ANY] * 3,
        out_specs=(ANY,) * 3,
        scratch_shapes=[
            pltpu.SemaphoreType.DMA((GATHER_COPIES,)),
            pltpu.SemaphoreType.DMA((GATHER_COPIES,)),
            pltpu.SemaphoreType.DMA((3,)),
        ],
        compiler_params=pltpu.CompilerParams(collective_id=0, has_side_effects=True),
        name="gather_blocks",
    )(row_packed, col_packed, sel)


LIVE, SLOT, OWNER, ROW, COL, ROW_FIRST, ROW_LAST, COL_FIRST, COL_USED = range(9)


def slots_kernel(plan, counts_ref, row_ref, col_ref, row_out, col_out, row_sum, col_sum, slope_ref):
    at = pl.program_id(0)
    block_items, features = row_sum.shape
    group = min(128, block_items)

    def offsets(ref):
        wide = ref[0, block_items:, :].astype(jnp.float32)
        pieces = [wide[i : i + 1] for i in range(block_items // features)]
        return pieces[0] if len(pieces) == 1 else jnp.concatenate(pieces, axis=1)

    @pl.when(at < plan[LIVE, 0])
    def _():
        col_vectors = col_ref[0, :block_items, :]
        row_shift = jnp.broadcast_to(offsets(row_ref), (8, block_items)).T[:, :1]
        col_shift = offsets(col_ref)
        for first in range(0, block_items, group):
            rows = slice(first, first + group)
            scores = lax.dot_general(
                row_ref[0, rows, :], col_vectors, (((1,), (1,)), ((), ())), preferred_element_type=jnp.float32
            )
            cells = counts_ref[0, rows, :].astype(jnp.float32)
            floored = jnp.maximum(cells, 1.0)
            gap = scores - row_shift[rows] - col_shift - jnp.log(floored)
            weight = conf_base + conf_scale * (floored * lax.rsqrt(floored))
            slope = jnp.where(cells > 0.0, weight * gap, 0.5 * jnp.tanh(0.5 * gap) + 0.5)
            slope_ref[rows, :] = slope.astype(jnp.bfloat16)
        slope = slope_ref[...]
        row_term = jnp.dot(slope, col_vectors, preferred_element_type=jnp.float32)

        @pl.when(plan[ROW_FIRST, at] == 1)
        def _():
            row_sum[...] = row_term

        @pl.when(plan[ROW_FIRST, at] == 0)
        def _():
            row_sum[...] += row_term

        @pl.when(plan[ROW_LAST, at] == 1)
        def _():
            row_out[0] = encode(row_sum[...])

        col_term = lax.dot_general(
            row_ref[0, :block_items, :], slope, (((0,), (0,)), ((), ())), preferred_element_type=jnp.float32
        )
        which = plan[COL, at]

        @pl.when(plan[COL_FIRST, at] == 1)
        def _():
            col_sum[which] = col_term

        @pl.when(plan[COL_FIRST, at] == 0)
        def _():
            col_sum[which] += col_term

    @pl.when(at == pl.num_programs(0) - 1)
    def _():
        def one(which, carry):
            @pl.when(plan[COL_USED, which] == 1)
            def _():
                col_out[which] = encode(col_sum[which])

            @pl.when(plan[COL_USED, which] == 0)
            def _():
                col_out[which] = jnp.zeros(col_out.shape[1:], jnp.int16)

            return carry

        lax.fori_loop(0, col_out.shape[0], one, 0)


def slots(plan, counts, row_pool, col_pool):
    count, block_items, unused = counts.shape
    owners, row_blocks, tall, features = row_pool.shape
    row_pool = row_pool.reshape(-1, tall, features)
    col_pool = col_pool.reshape(-1, tall, features)
    col_blocks = col_pool.shape[0]
    grid_spec = pltpu.PrefetchScalarGridSpec(
        num_scalar_prefetch=1,
        grid=(count,),
        in_specs=[
            pl.BlockSpec((1, block_items, block_items), lambda i, plan: (plan[SLOT, i], 0, 0)),
            pl.BlockSpec((1, tall, features), lambda i, plan: (plan[ROW, i], 0, 0)),
            pl.BlockSpec((1, tall, features), lambda i, plan: (plan[COL, i], 0, 0)),
        ],
        out_specs=(
            pl.BlockSpec((1, block_items, features), lambda i, plan: (plan[OWNER, i], 0, 0)),
            pl.BlockSpec((col_blocks, features, block_items), lambda i, plan: (0, 0, 0)),
        ),
        scratch_shapes=[
            pltpu.VMEM((block_items, features), jnp.float32),
            pltpu.VMEM((col_blocks, features, block_items), jnp.float32),
            pltpu.VMEM((block_items, block_items), jnp.bfloat16),
        ],
    )
    return pl.pallas_call(
        slots_kernel,
        out_shape=(
            jax.ShapeDtypeStruct((owners, block_items, features), jnp.int16),
            jax.ShapeDtypeStruct((col_blocks, features, block_items), jnp.int16),
        ),
        grid_spec=grid_spec,
        compiler_params=pltpu.CompilerParams(dimension_semantics=("arbitrary",)),
        name="slot_terms",
    )(plan, counts, row_pool, col_pool)


def reduce_kernel(
    row_terms, col_terms, sel_ref, row_embed, row_accum, col_embed, col_accum,
    row_out, col_out,
    stage, relay_one, row_sum, row_mid, relay_two, row_fin,
    col_own, col_part, col_sum, col_mid, relay_y, col_fin, state, fresh,
    send_sems, recv_sems, local_sems,
):
    x, z, y, core = place()
    half = row_terms.shape[2] // 2
    blocks, features, items = col_terms.shape[2:]
    ring = [device(turn(x, d), y, z, core) for d in (1, -1)] + [device(x, y, turn(z, d), core) for d in (1, -1)]
    along_y = [device(x, turn(y, d), z, core) for d in (1, -1)]
    partner = device(x, y, z, 1 - core)
    greet(ring + along_y + [partner])
    net = Copies(send_sems, recv_sems)
    here = ((x, z), (z, x))
    low, high, whole = pl.ds(0, 2), pl.ds(2, 2), pl.ds(0, SIDE)
    ways = ((1, low), (-1, high))

    def rows_of(way, first, second):
        piece = pl.ds(way * half, half)
        if way == 0:
            return row_terms.at[first, second, piece]
        return row_terms.at[second, first, piece]

    def to(way, stage_number, by):
        axis = way if stage_number == 0 else 1 - way
        if axis == 0:
            return device(turn(x, by), y, z, core)
        return device(x, y, turn(z, by), core)

    local = []

    def fetch(source, target):
        copy = pltpu.make_async_copy(source, target, local_sems.at[len(local)])
        copy.start()
        local.append(copy)
        return copy

    part, relayed, direct = {}, {}, {}
    for by in (2, 1, -1, 0):
        at = turn(y, by)
        part[by] = net.start(col_terms.at[at, 1 - core], col_part.at[at], partner)
    for way in (0, 1):
        p = here[way][0]
        for at, (by, pick) in enumerate(ways):
            relayed[way, by] = net.start(rows_of(way, turn(p, 2), pick), relay_one.at[way, at], to(way, 0, by))
    for way in (0, 1):
        p = here[way][0]
        for by in (1, -1):
            direct[way, by] = net.start(rows_of(way, turn(p, by), whole), stage.at[way, p], to(way, 0, by))
    own_cols = {by: fetch(col_terms.at[turn(y, by), core], col_own.at[turn(y, by)]) for by in (2, 1, -1, 0)}
    own_rows = [fetch(rows_of(way, here[way][0], whole), stage.at[way, here[way][0]]) for way in (0, 1)]
    loads = [fetch(ref, state.at[i]) for i, ref in enumerate((col_embed, col_accum, row_embed, row_accum))]

    tall = min(32, features)

    def over(count, size, body):
        @pl.loop(0, count)
        def _(i):
            body(pl.ds(pl.multiple_of(i * size, size), size))

    y_relay, y_direct = {}, {}
    for by in (2, 1, -1):
        at = turn(y, by)
        own_cols[by].wait()
        part[by].wait_recv()
        slot = (2, 1, -1).index(by)
        for block in range(blocks):
            def body(rows, block=block, at=at, slot=slot):
                both = decode(col_own[at, block, rows, :]) + decode(col_part[at, block, rows, :])
                col_mid[slot, block, rows, :] = encode(both)

            over(features // tall, tall, body)
        if by == 2:
            for i, way_y in enumerate((1, -1)):
                y_relay[way_y] = net.start(col_mid.at[slot, i], relay_y.at[i], along_y[i])
        else:
            y_direct[by] = net.start(col_mid.at[slot], col_fin.at[y], along_y[0 if by == 1 else 1])

    passed = {}
    for way in (0, 1):
        p = here[way][0]
        for at, (by, pick) in enumerate(ways):
            relayed[way, by].wait_recv()
            passed[way, by] = net.start(relay_one.at[way, at], stage.at[way, turn(p, -by), pick], to(way, 0, by))

    own_cols[0].wait()
    part[0].wait_recv()
    for block in range(blocks):
        def body(rows, block=block):
            col_sum[block, rows, :] = decode(col_own[y, block, rows, :]) + decode(col_part[y, block, rows, :])

        over(features // tall, tall, body)

    def gain(way, origin, second):
        p, q = here[way]
        first = turn(p, origin)
        holder = first * SIDE + q if way == 0 else q * SIDE + first
        owner = p * SIDE + second if way == 0 else second * SIDE + p
        chosen = sel_ref[holder, 0, owner]
        return [(chosen == block).astype(jnp.float32) for block in range(2)]

    step = min(32, half)

    def gather_sum(way, origin, dq, keep, finish):
        p, q = here[way]
        second = turn(q, dq)
        first = turn(p, origin)
        weights = gain(way, origin, second)

        def body(rows):
            term = decode(stage[way, first, second, rows, :])
            for block in range(2):
                value = term * weights[block]
                if keep:
                    value = value + row_sum[way, dq % SIDE, block, rows, :]
                if finish:
                    row_mid[way, dq % SIDE, block, rows, :] = encode(value)
                else:
                    row_sum[way, dq % SIDE, block, rows, :] = value

        over(half // step, step, body)

    for way in (0, 1):
        own_rows[way].wait()
        for dq in range(SIDE):
            gather_sum(way, 0, dq, False, False)
    y_pass = {}
    for i, by in enumerate((1, -1)):
        y_relay[by].wait_recv()
        y_pass[by] = net.start(relay_y.at[i], col_fin.at[turn(y, -by), i], along_y[i])
    for by in (1, -1):
        for way in (0, 1):
            direct[way, by].wait_recv()
            for dq in range(SIDE):
                gather_sum(way, -by, dq, True, False)
    row_relay, row_direct = {}, {}
    for way in (0, 1):
        q = here[way][1]
        for by in (1, -1):
            passed[way, by].wait_recv()
        for dq in (2, 1, 3):
            gather_sum(way, 2, dq, True, True)
            if dq == 2:
                for i, by in enumerate((1, -1)):
                    row_relay[way, by] = net.start(row_mid.at[way, 2, i], relay_two.at[way, i], to(way, 1, by))
            else:
                by = 1 if dq == 1 else -1
                row_direct[way, by] = net.start(row_mid.at[way, dq], row_fin.at[way, q], to(way, 1, by))
    for way in (0, 1):
        gather_sum(way, 2, 0, True, False)

    def add_cols(origin, block):
        at = turn(y, origin)

        def body(rows):
            col_sum[block, rows, :] += decode(col_fin[at, block, rows, :])

        over(features // tall, tall, body)

    for by in (1, -1):
        y_direct[by].wait_recv()
        for block in range(blocks):
            add_cols(-by, block)

    row_pass = {}
    for way in (0, 1):
        q = here[way][1]
        for i, by in enumerate((1, -1)):
            row_relay[way, by].wait_recv()
            row_pass[way, by] = net.start(relay_two.at[way, i], row_fin.at[way, turn(q, -by), i], to(way, 1, by))

    for i, by in enumerate((1, -1)):
        y_pass[by].wait_recv()
        add_cols(2, i)
    loads[0].wait()
    loads[1].wait()

    def renew(which, block, rows, grad):
        total = state[2 * which + 1, block, rows, :] + grad * grad
        fresh[which, block, rows, :] = state[2 * which, block, rows, :] - (learning_rate * grad) * lax.rsqrt(total)

    wide = min(128, items)
    for block in range(blocks):
        def body(rows, block=block):
            renew(0, block, rows, col_sum[block, :, rows].T)

        over(items // wide, wide, body)
    stores = [pltpu.make_async_copy(fresh.at[0], col_out, local_sems.at[len(local)])]
    stores[0].start()
    loads[2].wait()
    loads[3].wait()

    for by in (1, -1):
        for way in (0, 1):
            q = here[way][1]
            row_direct[way, by].wait_recv()
            at = turn(q, -by)
            for block in range(2):
                def body(rows, way=way, at=at, block=block):
                    row_sum[way, 0, block, rows, :] += decode(row_fin[way, at, block, rows, :])

                over(half // step, step, body)
    for way in (0, 1):
        q = here[way][1]
        for i, by in enumerate((1, -1)):
            row_pass[way, by].wait_recv()
            at = turn(q, 2)

            @pl.loop(0, half // step)
            def _(n, way=way, at=at, block=i):
                rows = pl.ds(pl.multiple_of(n * step, step), step)
                grad = row_sum[way, 0, block, rows, :] + decode(row_fin[way, at, block, rows, :])
                renew(1, block, pl.ds(pl.multiple_of(way * half + n * step, step), step), grad)

    stores.append(pltpu.make_async_copy(fresh.at[1], row_out, local_sems.at[len(local) + 1]))
    stores[1].start()
    net.finish()
    for copy in stores:
        copy.wait()


REDUCE_COPIES = 4 + 4 + 4 + 2 + 2 + 4 + 2 + 4 + 4 + 4


def reduce_terms(row_terms, col_terms, sel_in, row_embed, row_accum, col_embed, col_accum):
    block_items, features = row_terms.shape[2:]
    half = block_items // 2
    wire, f32 = jnp.int16, jnp.float32
    col_block = col_terms.shape[2:]
    state = row_embed.shape
    shape = jax.ShapeDtypeStruct(state, f32)
    return pl.pallas_call(
        reduce_kernel,
        out_shape=(shape, shape),
        in_specs=[ANY] * 2 + [pl.BlockSpec(memory_space=pltpu.SMEM)] + [ANY] * 4,
        out_specs=(ANY,) * 2,
        scratch_shapes=[
            pltpu.VMEM((2, SIDE, SIDE, half, features), wire),
            pltpu.VMEM((2, 2, 2, half, features), wire),
            pltpu.VMEM((2, SIDE, 2, half, features), f32),
            pltpu.VMEM((2, SIDE, 2, half, features), wire),
            pltpu.VMEM((2, 2, half, features), wire),
            pltpu.VMEM((2, SIDE, 2, half, features), wire),
            pltpu.VMEM((SIDE,) + col_block, wire),
            pltpu.VMEM((SIDE,) + col_block, wire),
            pltpu.VMEM(col_block, f32),
            pltpu.VMEM((3,) + col_block, wire),
            pltpu.VMEM((2,) + col_block[1:], wire),
            pltpu.VMEM((SIDE,) + col_block, wire),
            pltpu.VMEM((4,) + state, f32),
            pltpu.VMEM((2,) + state, f32),
            pltpu.SemaphoreType.DMA((REDUCE_COPIES,)),
            pltpu.SemaphoreType.DMA((REDUCE_COPIES,)),
            pltpu.SemaphoreType.DMA((12,)),
        ],
        compiler_params=pltpu.CompilerParams(collective_id=1, has_side_effects=True),
        name="reduce_terms",
    )(row_terms, col_terms, sel_in, row_embed, row_accum, col_embed, col_accum)


def prepare_kernel(
    rows_ref, cols_ref, listed_ref, row_embed, row_shift, col_embed, col_shift,
    row_packed, col_packed, plan_ref, sel_ref, *, row_blocks, col_blocks,
):
    count = rows_ref.shape[0]
    around, owners = SIDE * 2, SIDE * SIDE
    live = listed_ref[0]
    lane = lax.broadcasted_iota(jnp.int32, (count, 128), 1)
    line = lax.broadcasted_iota(jnp.int32, (count, 128), 0)
    zero = jnp.zeros((count, 128), jnp.int32)
    lists = {"owner": [zero, zero], "block": [zero, zero], "col": [zero, zero]}
    for i in range(count):
        r, c = rows_ref[i], cols_ref[i]
        values = {
            "owner": r // (row_blocks * around),
            "block": r % row_blocks,
            "col": c // col_blocks % around * col_blocks + c % col_blocks,
        }
        for name, (down, across) in lists.items():
            lists[name] = [jnp.where(line == i, values[name], down), jnp.where(lane == i, values[name], across)]
    owner, owner_l = lists["owner"]
    block, unused = lists["block"]
    col, col_l = lists["col"]
    listed, listed_l = line < live, lane < live
    key = jnp.where(listed, owner, owners) * count + line
    key_l = jnp.where(listed_l, owner_l, owners) * count + lane

    def tally(truth, axis):
        return jnp.sum(jnp.where(truth, 1.0, 0.0), axis=axis, keepdims=True)

    rank = tally((key_l < key) & (lane < count), 1).astype(jnp.int32)
    mine = (owner_l == owner) & listed_l
    row_first = tally(mine & (key_l < key), 1) == 0.0
    row_last = tally(mine & (key_l > key), 1) == 0.0
    col_first = tally((col_l == col) & listed_l & (key_l < key), 1) == 0.0
    takes = rank == jnp.minimum(lane, live - 1)

    def ordered(value):
        return jnp.sum(jnp.where(takes, value, 0).astype(jnp.float32), axis=0, keepdims=True).astype(jnp.int32)

    plan_ref[...] = jnp.zeros_like(plan_ref)
    plan_ref[LIVE : LIVE + 1, :] = jnp.full((1, 128), live, jnp.int32)
    plan_ref[SLOT : SLOT + 1, :] = ordered(line)
    plan_ref[OWNER : OWNER + 1, :] = ordered(owner)
    plan_ref[ROW : ROW + 1, :] = ordered(owner * row_blocks + block)
    plan_ref[COL : COL + 1, :] = ordered(col)
    plan_ref[ROW_FIRST : ROW_FIRST + 1, :] = ordered(jnp.where(row_first, 1, zero))
    plan_ref[ROW_LAST : ROW_LAST + 1, :] = ordered(jnp.where(row_last, 1, zero))
    plan_ref[COL_FIRST : COL_FIRST + 1, :] = ordered(jnp.where(col_first, 1, zero))
    plan_ref[COL_USED : COL_USED + 1, :] = jnp.where(tally((col == lane) & listed, 0) > 0.0, 1, 0)
    hit = (owner == lane) & listed
    chosen = jnp.min(jnp.where(hit, block, row_blocks).astype(jnp.float32), axis=0, keepdims=True)
    sel_ref[...] = jnp.broadcast_to(chosen, (8, 128)).astype(jnp.int32)

    for embed, shift, packed in ((row_embed, row_shift, row_packed), (col_embed, col_shift, col_packed)):
        blocks, tall, features = packed.shape
        items = tall - PAD
        for at in range(blocks):
            packed[at, :items, :] = embed[at * items : (at + 1) * items, :].astype(jnp.bfloat16)
            wide = jnp.zeros((PAD, features), jnp.float32)
            place_at = lax.broadcasted_iota(jnp.int32, (PAD, features), 0)
            for i in range(items // features):
                n = at * (items // features) + i
                wide = jnp.where(place_at == i, shift[n : n + 1, :].astype(jnp.float32), wide)
            packed[at, items:, :] = wide.astype(jnp.bfloat16)


def prepare(shard_rows, shard_cols, listed, row_embed, row_offset, col_embed, col_offset, block_items):
    features = row_embed.shape[1]
    row_blocks, col_blocks = row_embed.shape[0] // block_items, col_embed.shape[0] // block_items
    scalars, vectors = pl.BlockSpec(memory_space=pltpu.SMEM), pl.BlockSpec(memory_space=pltpu.VMEM)
    return pl.pallas_call(
        functools.partial(prepare_kernel, row_blocks=row_blocks, col_blocks=col_blocks),
        out_shape=(
            jax.ShapeDtypeStruct((row_blocks, block_items + PAD, features), jnp.bfloat16),
            jax.ShapeDtypeStruct((col_blocks, block_items + PAD, features), jnp.bfloat16),
            jax.ShapeDtypeStruct((16, 128), jnp.int32),
            jax.ShapeDtypeStruct((8, 128), jnp.int32),
        ),
        in_specs=[scalars] * 3 + [vectors] * 4,
        out_specs=(vectors,) * 4,
        name="prepare",
    )(
        shard_rows,
        shard_cols,
        listed,
        row_embed,
        row_offset.reshape(-1, features),
        col_embed,
        col_offset.reshape(-1, features),
    )


def on_device(
    counts, shard_rows, shard_cols, listed, row_embed, row_accum, row_offset, col_embed, col_accum, col_offset
):
    block_items = counts.shape[1]
    features = row_embed.shape[1]
    row_blocks = row_embed.shape[0] // block_items
    col_blocks = col_embed.shape[0] // block_items
    row_packed, col_packed, plan, sel = prepare(
        shard_rows, shard_cols, listed, row_embed, row_offset, col_embed, col_offset, block_items
    )
    row_pool, col_pool, sel_in = gather(row_packed, col_packed, sel)
    row_terms, col_terms = slots(plan, counts, row_pool, col_pool)
    row_state = (row_blocks, block_items, features)
    col_state = (col_blocks, block_items, features)
    row_new, col_new = reduce_terms(
        row_terms.reshape(SIDE, SIDE, block_items, features),
        col_terms.reshape(SIDE, 2, col_blocks, features, block_items),
        sel_in,
        row_embed.reshape(row_state),
        row_accum.reshape(row_state),
        col_embed.reshape(col_state),
        col_accum.reshape(col_state),
    )
    return (row_new.reshape(row_embed.shape), col_new.reshape(col_embed.shape))


def solution(mesh):
    devices = ("rows", "cols")
    in_specs = (P(devices, None, None), P(devices), P(devices), P(devices)) + (
        P(devices, None),
        P(devices, None),
        P(devices),
    ) * 2
    out_specs = (P(devices, None), P(devices, None))
    return jax.shard_map(on_device, mesh=mesh, in_specs=in_specs, out_specs=out_specs, check_vma=False)
```
